32 devices in a mesh: gx: 4 (over y, x), gy: 8 (over z, core).
Axes of the slice: x: 2, y: 2, z: 4, core: 2. Of those that a mesh axis runs over, the one named last changes fastest.
Arguments:
- schur_blocks: float32 [32, 2048, 2048], P(('gx', 'gy')), may hold values from -1 to 11, as said below
- offsets: int32 [32], P(('gx', 'gy')), may hold values from 256 to 768, as said below
- right_side: float32 [32768, 128], P(('gx', 'gy')), may hold values from -20 to 20
- coarse_basis: float32 [32768, 128], P(('gx', 'gy')), may hold values from -0.03125 to 0.03125
- coarse_load: float32 [128, 128], replicated, may hold values from -6 to 6
Outputs:
- multipliers: float32 [32768, 128], P(('gx', 'gy'))
- amplitudes: float32 [128, 128], replicated
The draws below stay inside these ranges and needn't reach their ends.
Inputs may be any that keep to these rules, and one draw needn't show every extreme that they name: `schur_blocks`: each block is symmetric positive definite. `offsets`: both ends of the range are taken by some subdomain.
All inputs are finite; a program needn't handle non-finite values.
Results may differ from the reference program's by a relative error of at most 0.0003.
Values sent between devices are 32-bit elements; how exact they have to be, the bound alone decides.
A program may use at most 128 MiB of HBM per device.

```python
import math
import jax
import jax.numpy as jnp
from jax import lax

W = 2048
SLAB = 1024
R = 128
NC = 128
ITERS = 3
SUBDOMAINS = 32
MULTS = 32768


def draw_schur_blocks(key, part):
    upper_end = 4.0
    subkeys = jax.random.split(key, SUBDOMAINS)

    def single(subkey):
        diag_key, noise_key = jax.random.split(subkey)
        diagonal = jnp.exp(jax.random.uniform(diag_key, (W,), jnp.float32, 0.0, math.log(upper_end)))
        noise_part = jax.random.truncated_normal(noise_key, -5.0, 5.0, (W, W), jnp.float32) * (0.25 / math.sqrt(W))
        return jnp.diag(diagonal) + (noise_part + noise_part.T) * 0.7071067811865476
    return lax.map(single, subkeys)


def draw_offsets(key, part):
    key_values, key_ranking = jax.random.split(key)
    lowest = SLAB // 4
    highest = 3 * SLAB // 4
    values = jax.random.randint(key_values, (SUBDOMAINS,), lowest, highest + 1).astype(jnp.int32)
    ranking = jax.random.permutation(key_ranking, SUBDOMAINS)
    values = values.at[ranking[0]].set(lowest).at[ranking[1]].set(highest)
    return values.astype(jnp.int32)


def draw_right_side(key, part):
    base_key = jax.random.fold_in(key, 0)
    total_rows = SLAB * SUBDOMAINS
    position = jnp.arange(total_rows, dtype=jnp.float32) / total_rows
    base = jax.random.truncated_normal(base_key, -4.0, 4.0, (total_rows, R), jnp.float32)
    rising = 1.0 + 2.0 * position
    return base * rising[:, None]


def block_scale(stream_key, dims, cuts, low, top_value):
    gain, own = 1.0, jax.random.fold_in(stream_key, 6)
    for dim, shards_of in cuts:
        heights = jnp.exp(jax.random.uniform(jax.random.fold_in(own, dim), (shards_of,), jnp.float32, low / len(cuts), top_value / len(cuts)))
        gain = gain * jnp.repeat(heights, dims[dim] // shards_of).reshape([-1 if axis == dim else 1 for axis in range(len(dims))])
    return gain


def gaussian(stream_key, extent, spread, reach, pieces=(), kind=jnp.bfloat16):
    values = jax.random.normal(stream_key, extent, jnp.float32) * spread
    if len(pieces) > 0:
        values = block_scale(stream_key, extent, pieces, -0.22, 0.18) * values
    return jnp.clip(values, min=-reach, max=reach).astype(kind)


def setup_inputs(seed: int = 0) -> dict:
    keys = jax.random.split(jax.random.key(seed), 6)
    return {
        "schur_blocks": draw_schur_blocks(jax.random.fold_in(keys[5], 71), 0),
        "offsets": draw_offsets(jax.random.fold_in(keys[5], 71), 0),
        "right_side": draw_right_side(jax.random.fold_in(keys[5], 71), 0),
        "coarse_basis": gaussian(keys[3], (MULTS, NC), MULTS ** -0.5, 0.03125, ((0, 32),), jnp.float32),
        "coarse_load": gaussian(keys[4], (NC, R), 1.0, 6.0, (), jnp.float32),
    }


HIGHEST = lax.Precision.HIGHEST

def apply_operator(vector, schur_blocks, offsets):
    padded = jnp.pad(vector, ((SLAB, SLAB), (0, 0)))

    def visit_block(accumulated, inputs):
        schur_block, start_row, device_index = inputs
        first_row = (device_index * SLAB + start_row).astype(jnp.int32)
        window = lax.dynamic_slice_in_dim(padded, first_row, W, 0)
        product_block = jnp.dot(schur_block.astype(jnp.float32), window.astype(jnp.float32), precision=HIGHEST, preferred_element_type=jnp.float32)
        current = lax.dynamic_slice_in_dim(accumulated, first_row, W, 0)
        return (lax.dynamic_update_slice_in_dim(accumulated, current + product_block, first_row, 0), None)
    indices = jnp.arange(SUBDOMAINS, dtype=jnp.int32)
    accumulated, _ = lax.scan(visit_block, jnp.zeros_like(padded), (schur_blocks, offsets.astype(jnp.int32), indices))
    return accumulated[SLAB:SLAB + vector.shape[0]]

def project(residual, coarse_basis, gram_factor):
    coarse_part = jnp.dot(coarse_basis.T.astype(jnp.float32), residual.astype(jnp.float32), precision=HIGHEST, preferred_element_type=jnp.float32)
    amplitudes = jax.scipy.linalg.cho_solve((gram_factor, True), coarse_part)
    projected = residual - jnp.dot(coarse_basis.astype(jnp.float32), amplitudes.astype(jnp.float32), precision=HIGHEST, preferred_element_type=jnp.float32)
    return (projected, amplitudes)

def reference(schur_blocks, offsets, right_side, coarse_basis, coarse_load):
    gram_matrix = jnp.dot(coarse_basis.T.astype(jnp.float32), coarse_basis.astype(jnp.float32), precision=HIGHEST, preferred_element_type=jnp.float32)
    gram_factor = jnp.linalg.cholesky(gram_matrix)
    start_load = jax.scipy.linalg.cho_solve((gram_factor, True), coarse_load)
    multipliers = jnp.dot(coarse_basis.astype(jnp.float32), start_load.astype(jnp.float32), precision=HIGHEST, preferred_element_type=jnp.float32)
    residual = right_side - apply_operator(multipliers, schur_blocks, offsets)
    projected, amplitudes = project(residual, coarse_basis, gram_factor)
    direction = projected
    energy_now = jnp.sum(projected * projected, axis=0)
    for iteration in range(ITERS):
        operator_image = apply_operator(direction, schur_blocks, offsets)
        step_length = energy_now / jnp.sum(direction * operator_image, axis=0)
        multipliers = multipliers + step_length * direction
        residual = residual - step_length * operator_image
        projected, amplitudes = project(residual, coarse_basis, gram_factor)
        energy_next = jnp.sum(projected * projected, axis=0)
        direction = projected + energy_next / energy_now * direction
        energy_now = energy_next
    return (multipliers, amplitudes)
```

```python
import functools

import jax
import jax.numpy as jnp
from jax import lax
from jax.experimental import pallas as pl
from jax.experimental.pallas import tpu as pltpu
from jax.sharding import PartitionSpec as P

ITERS = 3
MESH = pl.DeviceIdType.MESH
HIGHEST = lax.Precision.HIGHEST
F32 = jnp.float32
BF16 = jnp.bfloat16
CHUNK = 128
SLOTS = 4
BLOCK = 512
EXCHANGES = 2 * ITERS + 2
REDUCES = 2 + ITERS


def dot(a, b):
    return jnp.dot(a, b, precision=HIGHEST, preferred_element_type=F32)


def kernel(
    nx, ny, off_ref, schur_ref, right_ref, basis_ref, load_ref, lam_ref, amp_ref,
    stage, s_hi, s_lo, vec, twice, basis_w, basis_t, fc_own, fc_w, fc_t, right_w, z, d, p_old, image_old, own,
    out_l, out_r, in_l, in_r, part, fold, total, m_ref, sweep, scal_in, scal_all,
    stage_sem, hs_l, hs_r, hr_l, hr_r, fold_s, fold_r, tot_s, tot_r, scal_s, scal_r,
):
    n = nx * ny
    slab = right_ref.shape[0]
    nc = basis_ref.shape[1]
    width = 2 * slab
    low = slab // 4
    span = slab - low
    me = lax.axis_index("gx") * ny + lax.axis_index("gy")
    off = off_ref[0]
    chunks = width // CHUNK

    def where_is(i):
        return (lax.div(i, ny), lax.rem(i, ny))

    def fetch(i, slot):
        return pltpu.make_async_copy(
            schur_ref.at[pl.ds(i * CHUNK, CHUNK), :], stage.at[slot], stage_sem.at[slot]
        )

    for i in range(SLOTS):
        fetch(i, i).start()

    @pl.when(me == 0)
    def _():
        in_l[...] = jnp.zeros_like(in_l)

    @pl.when(me == n - 1)
    def _():
        in_r[...] = jnp.zeros_like(in_r)

    barrier = pltpu.get_barrier_semaphore()

    def greet(k, carry):
        pl.semaphore_signal(barrier, inc=1, device_id=where_is(lax.rem(me + k, n)), device_id_type=MESH)
        return carry

    lax.fori_loop(1, n, greet, 0)
    pl.semaphore_wait(barrier, n - 1)

    def to_right(e, src):
        return pltpu.make_async_remote_copy(
            src_ref=src, dst_ref=in_l.at[e], send_sem=hs_r.at[e], recv_sem=hr_l.at[e],
            device_id=where_is(lax.rem(me + 1, n)), device_id_type=MESH,
        )

    def to_left(e, src):
        return pltpu.make_async_remote_copy(
            src_ref=src, dst_ref=in_r.at[e], send_sem=hs_l.at[e], recv_sem=hr_r.at[e],
            device_id=where_is(lax.rem(me + n - 1, n)), device_id_type=MESH,
        )

    def send_halo(e, src_l, src_r):
        @pl.when(me > 0)
        def _():
            to_left(e, src_l).start()

        @pl.when(me < n - 1)
        def _():
            to_right(e, src_r).start()

    def wait_halo(e):
        @pl.when(me > 0)
        def _():
            to_right(e, out_r.at[0]).wait_recv()

        @pl.when(me < n - 1)
        def _():
            to_left(e, out_l.at[0]).wait_recv()

    def wait_sent(e):
        @pl.when(me > 0)
        def _():
            to_left(e, out_l.at[0]).wait_send()

        @pl.when(me < n - 1)
        def _():
            to_right(e, out_r.at[0]).wait_send()

    def rows_below(first, count):
        return lax.broadcasted_iota(jnp.int32, (count, nc), 0) + first < off

    def folded_halo(e, first, count):
        mask = rows_below(first, count)
        right = in_r[e, pl.ds(first, count), :] if first + count <= span else jnp.zeros((count, nc), F32)
        left = in_l[e, pl.ds(first - low, count), :] if first >= low else jnp.zeros((count, nc), F32)
        return jnp.where(mask, right, left)

    def folded(e):
        return jnp.concatenate([folded_halo(e, i * low, low) for i in range(slab // low)], axis=0)

    def apply_block(src):
        twice[0:width, :] = src[...]
        twice[width:, :] = src[...]
        window = twice[pl.ds(off, width), :]
        hi = window.astype(BF16)
        vec[:, :nc] = hi
        vec[:, nc:] = (window - hi.astype(F32)).astype(BF16)

        def rows(i, carry):
            at = pl.ds(pl.multiple_of(i * BLOCK, BLOCK), BLOCK)
            both = jnp.dot(s_hi[at, :], vec[...], preferred_element_type=F32)
            rest = jnp.dot(s_lo[at, :], vec[:, :nc], preferred_element_type=F32)
            result = both[:, :nc] + (both[:, nc:] + rest)
            twice[at, :] = result
            twice[pl.ds(pl.multiple_of(width + i * BLOCK, BLOCK), BLOCK), :] = result
            return carry

        lax.fori_loop(0, width // BLOCK, rows, 0)

    def folded_product():
        return twice[pl.ds(width - off, width), :]

    def send_parts(e, k, product):
        mask = rows_below(0, slab)
        head = product[:slab]
        out_l[k] = jnp.where(mask, 0.0, head)[low:]
        out_r[k] = jnp.where(mask, head, 0.0)[:span]
        send_halo(e, out_l.at[k], out_r.at[k])

    def assemble(e, product):
        wait_halo(e)
        left = in_l[e]
        right = in_r[e]
        mine = product[slab:]
        return jnp.concatenate(
            [
                mine[:low] + left[:low],
                mine[low:span] + (left[low:] + right[: span - low]),
                mine[span:] + right[span - low :],
            ],
            axis=0,
        )

    def reduce_start(r, value):
        rows = value.shape[0]
        p = rows // n
        for i in range(n):
            part[r][i] = value[i * p : (i + 1) * p]

        def send(k, carry):
            peer = lax.rem(me + k, n)
            pltpu.make_async_remote_copy(
                src_ref=part[r].at[peer], dst_ref=fold[r].at[me], send_sem=fold_s.at[r],
                recv_sem=fold_r.at[r], device_id=where_is(peer), device_id_type=MESH,
            ).start()
            return carry

        lax.fori_loop(1, n, send, 0)
        fold[r][me] = part[r][me]

    def reduce_turn(r):
        arrived = fold[r].at[pl.ds(0, n - 1)]
        pltpu.make_async_copy(arrived, arrived, fold_r.at[r]).wait()
        total[r][me] = jnp.sum(fold[r][...], axis=0)

        def send(k, carry):
            peer = lax.rem(me + k, n)
            pltpu.make_async_remote_copy(
                src_ref=total[r].at[me], dst_ref=total[r].at[me], send_sem=tot_s.at[r],
                recv_sem=tot_r.at[r], device_id=where_is(peer), device_id_type=MESH,
            ).start()
            return carry

        lax.fori_loop(1, n, send, 0)

    def reduce_end(r):
        arrived = total[r].at[pl.ds(0, n - 1)]
        pltpu.make_async_copy(arrived, arrived, tot_r.at[r]).wait()
        p = total[r].shape[1]
        for i in range(n):
            m_ref[i * p : (i + 1) * p, :] = total[r][i]
        return m_ref[: n * p, :]

    def scal_start(it):
        scal_all[it, me] = scal_in[it]

        def send(k, carry):
            peer = lax.rem(me + k, n)
            pltpu.make_async_remote_copy(
                src_ref=scal_in.at[it], dst_ref=scal_all.at[it, me], send_sem=scal_s.at[it],
                recv_sem=scal_r.at[it], device_id=where_is(peer), device_id_type=MESH,
            ).start()
            return carry

        lax.fori_loop(1, n, send, 0)

    def scal_end(it):
        arrived = scal_all.at[it, pl.ds(0, n - 1)]
        pltpu.make_async_copy(arrived, arrived, scal_r.at[it]).wait()
        sums = jnp.sum(scal_all[it], axis=0)
        return sums[0:1], sums[1:2], sums[2:3]

    send_halo(0, basis_ref.at[pl.ds(0, span)], basis_ref.at[pl.ds(low, span)])
    send_halo(1, right_ref.at[pl.ds(0, span)], right_ref.at[pl.ds(low, span)])
    basis_t[...] = basis_ref[...].T
    both = jnp.concatenate([basis_ref[...], right_ref[...]], axis=1)
    local = dot(basis_t[...], both)
    reduce_start(0, jnp.concatenate([local[:, :nc], local[:, nc:]], axis=0))

    def split(i, carry):
        slot = lax.rem(i, SLOTS)
        fetch(i, slot).wait()
        at = pl.ds(pl.multiple_of(i * CHUNK, CHUNK), CHUNK)
        value = stage[slot]
        hi = value.astype(BF16)
        s_hi[at, :] = hi
        s_lo[at, :] = (value - hi.astype(F32)).astype(BF16)

        @pl.when(i + SLOTS < chunks)
        def _():
            fetch(i + SLOTS, slot).start()

        return carry

    lax.fori_loop(0, chunks, split, 0)
    reduce_turn(0)

    wait_halo(0)
    basis_w[0:slab, :] = folded(0)
    basis_w[slab:, :] = basis_ref[...]
    apply_block(basis_w)
    product = folded_product()
    send_parts(2, 0, product)
    fc_own[...] = assemble(2, product)
    send_halo(3, fc_own.at[pl.ds(0, span)], fc_own.at[pl.ds(low, span)])
    reduce_start(1, dot(basis_t[...], fc_own[...]))
    fc_t[...] = fc_own[...].T
    gram = reduce_end(0)
    sweep[...] = gram[:nc]
    right_coarse = gram[nc:]
    reduce_turn(1)

    lanes = lax.broadcasted_iota(jnp.int32, (nc, nc), 1)
    subs = lax.broadcasted_iota(jnp.int32, (nc, nc), 0)

    def pivot(k, a):
        row = sweep[pl.ds(k, 1), :]
        here = lanes == k
        col = jnp.sum(jnp.where(here, a, 0.0), axis=1, keepdims=True)
        inverse = 1.0 / jnp.sum(jnp.where(lanes[:1] == k, row, 0.0), axis=1, keepdims=True)
        scaled = row * inverse
        new = a - col * scaled
        new = jnp.where(here, col * inverse, new)
        new = jnp.where(subs == k, jnp.where(here, -inverse, scaled), new)
        sweep[...] = new
        return new

    ginv = -lax.fori_loop(0, nc, pivot, sweep[...])

    y0 = dot(ginv, load_ref[...])
    lam_ref[...] = dot(basis_ref[...], y0)
    cfc = reduce_end(1)
    amp = dot(ginv, right_coarse - dot(cfc, y0))
    wait_halo(1)
    wait_halo(3)
    right_w[0:slab, :] = folded(1)
    right_w[slab:, :] = right_ref[...]
    fc_w[0:slab, :] = folded(3)
    fc_w[slab:, :] = fc_own[...]
    z[...] = right_w[...] - dot(fc_w[...], y0) - dot(basis_w[...], amp)

    energy = curvature = coarse_image = None
    for it in range(ITERS):
        last = it == ITERS - 1
        reduce_start(2 + it, dot(fc_t[...], z[slab:, :]))
        apply_block(z)
        product = folded_product()
        e = 4 + 2 * it
        if not last:
            send_parts(e, 1 + it, product)
        scal_in[it, 0:1] = jnp.sum(z[...] * product, axis=0, keepdims=True)
        scal_in[it, 1:2] = jnp.sum(z[slab:, :] * z[slab:, :], axis=0, keepdims=True)
        if it == 0:
            scal_in[it, 2:3] = jnp.zeros((1, nc), F32)
        else:
            scal_in[it, 2:3] = jnp.sum(z[...] * p_old[...], axis=0, keepdims=True)
        scal_in[it, 3:4] = jnp.zeros((1, nc), F32)
        scal_start(it)
        reduce_turn(2 + it)
        if not last:
            own[it] = assemble(e, product)
            send_halo(e + 1, own.at[it, pl.ds(0, span)], own.at[it, pl.ds(low, span)])
        curved, energy_now, crossed = scal_end(it)
        coarse_now = reduce_end(2 + it)
        if it == 0:
            d[...] = z[slab:, :]
            curvature = curved
            coarse_image = coarse_now
            if not last:
                p_old[...] = product
        else:
            beta = energy_now / energy
            d[...] = z[slab:, :] + beta * d[...]
            curvature = curved + beta * (2.0 * crossed + beta * curvature)
            coarse_image = coarse_now + beta * coarse_image
            if not last:
                p_old[...] = product + beta * p_old[...]
        energy = energy_now
        step = energy / curvature
        lam_ref[...] += step * d[...]
        shift = dot(ginv, coarse_image)
        amp = amp - step * shift
        if not last:
            wait_halo(e + 1)
            whole = jnp.concatenate([folded(e + 1), own[it]], axis=0)
            if it > 0:
                whole = whole + beta * image_old[...]
            image_old[...] = whole
            z[...] = z[...] - step * (whole - dot(basis_w[...], shift))
    amp_ref[...] = amp

    for e in range(EXCHANGES):
        wait_sent(e)
    for r in range(REDUCES):
        sent = fold[r].at[pl.ds(0, n - 1)]
        pltpu.make_async_copy(sent, sent, fold_s.at[r]).wait()
        sent = total[r].at[pl.ds(0, n - 1)]
        pltpu.make_async_copy(sent, sent, tot_s.at[r]).wait()
    for it in range(ITERS):
        sent = scal_all.at[it, pl.ds(0, n - 1)]
        pltpu.make_async_copy(sent, sent, scal_s.at[it]).wait()


def entry(nx, ny, groups, *refs):
    fixed = refs[: groups[0]]
    rest = refs[groups[0] :]
    part, rest = rest[:REDUCES], rest[REDUCES:]
    fold, rest = rest[:REDUCES], rest[REDUCES:]
    total, rest = rest[:REDUCES], rest[REDUCES:]
    kernel(nx, ny, *fixed, part, fold, total, *rest)


def solution(mesh):
    nx, ny = mesh.shape["gx"], mesh.shape["gy"]
    n = nx * ny

    def local(schur_blocks, offsets, right_side, coarse_basis, coarse_load):
        slab, r = right_side.shape
        nc = coarse_basis.shape[1]
        width = schur_blocks.shape[1]
        span = slab - slab // 4
        row_counts = [2 * nc] + [nc] * (REDUCES - 1)

        def pieces():
            return [pltpu.VMEM((n, rows // n, r), F32) for rows in row_counts]

        vmem = pl.BlockSpec(memory_space=pltpu.VMEM)
        fixed = [
            pltpu.VMEM((SLOTS, CHUNK, width), F32),
            pltpu.VMEM((width, width), BF16),
            pltpu.VMEM((width, width), BF16),
            pltpu.VMEM((width, 2 * r), BF16),
            pltpu.VMEM((2 * width, r), F32),
            pltpu.VMEM((width, nc), F32),
            pltpu.VMEM((nc, slab), F32),
            pltpu.VMEM((slab, nc), F32),
            pltpu.VMEM((width, nc), F32),
            pltpu.VMEM((nc, slab), F32),
            pltpu.VMEM((width, r), F32),
            pltpu.VMEM((width, r), F32),
            pltpu.VMEM((slab, r), F32),
            pltpu.VMEM((width, r), F32),
            pltpu.VMEM((width, r), F32),
            pltpu.VMEM((ITERS - 1, slab, r), F32),
            pltpu.VMEM((ITERS, span, r), F32),
            pltpu.VMEM((ITERS, span, r), F32),
            pltpu.VMEM((EXCHANGES, span, r), F32),
            pltpu.VMEM((EXCHANGES, span, r), F32),
        ]
        dma = pltpu.SemaphoreType.DMA
        rest = [
            pltpu.VMEM((2 * nc, r), F32),
            pltpu.VMEM((nc, nc), F32),
            pltpu.VMEM((ITERS, 4, r), F32),
            pltpu.VMEM((ITERS, n, 4, r), F32),
            dma((SLOTS,)),
            dma((EXCHANGES,)), dma((EXCHANGES,)), dma((EXCHANGES,)), dma((EXCHANGES,)),
            dma((REDUCES,)), dma((REDUCES,)), dma((REDUCES,)), dma((REDUCES,)),
            dma((ITERS,)), dma((ITERS,)),
        ]
        return pl.pallas_call(
            functools.partial(entry, nx, ny, (7 + len(fixed),)),
            out_shape=(
                jax.ShapeDtypeStruct((slab, r), F32),
                jax.ShapeDtypeStruct((nc, r), F32),
            ),
            in_specs=[
                pl.BlockSpec(memory_space=pltpu.SMEM),
                pl.BlockSpec(memory_space=pl.ANY),
                vmem, vmem, vmem,
            ],
            out_specs=(vmem, vmem),
            scratch_shapes=fixed + pieces() + pieces() + pieces() + rest,
            compiler_params=pltpu.CompilerParams(
                collective_id=0, has_side_effects=True, vmem_limit_bytes=60 * 1024 * 1024
            ),
            name="projected_cg",
        )(offsets, schur_blocks[0], right_side, coarse_basis, coarse_load)

    in_specs = (
        P(("gx", "gy"), None, None),
        P(("gx", "gy")),
        P(("gx", "gy"), None),
        P(("gx", "gy"), None),
        P(),
    )
    out_specs = (P(("gx", "gy"), None), P())
    return jax.shard_map(local, mesh=mesh, in_specs=in_specs, out_specs=out_specs, check_vma=False)
```

```python
import functools

import jax
import jax.numpy as jnp
from jax import lax
from jax.experimental import pallas as pl
from jax.experimental.pallas import tpu as pltpu
from jax.sharding import PartitionSpec as P

ITERS = 3
MESH = pl.DeviceIdType.MESH
HIGHEST = lax.Precision.HIGHEST
F32 = jnp.float32
BF16 = jnp.bfloat16
CHUNK = 128
SLOTS = 4
BLOCK = 512
EXCHANGES = 2 * ITERS + 2
REDUCES = 2 + ITERS


def dot(a, b):
    return jnp.dot(a, b, precision=HIGHEST, preferred_element_type=F32)


def kernel(
    nx, ny, off_ref, schur_ref, right_ref, basis_ref, load_ref, lam_ref, amp_ref,
    stage, s_hi, s_lo, vec, twice, basis_w, basis_t, fc_own, fc_w, fc_t, right_w, z, d, p_old, image_old, own,
    out_l, out_r, in_l, in_r, part, fold, total, m_ref, sweep, scal_in, scal_all,
    stage_sem, hs_l, hs_r, hr_l, hr_r, fold_s, fold_r, tot_s, tot_r, scal_s, scal_r,
):
    n = nx * ny
    slab = right_ref.shape[0]
    nc = basis_ref.shape[1]
    width = 2 * slab
    low = slab // 4
    span = slab - low
    me = lax.axis_index("gx") * ny + lax.axis_index("gy")
    off = off_ref[0]
    chunks = width // CHUNK

    def where_is(i):
        return (lax.div(i, ny), lax.rem(i, ny))

    def fetch(i, slot):
        return pltpu.make_async_copy(
            schur_ref.at[pl.ds(i * CHUNK, CHUNK), :], stage.at[slot], stage_sem.at[slot]
        )

    for i in range(SLOTS):
        fetch(i, i).start()

    @pl.when(me == 0)
    def _():
        in_l[...] = jnp.zeros_like(in_l)

    @pl.when(me == n - 1)
    def _():
        in_r[...] = jnp.zeros_like(in_r)

    barrier = pltpu.get_barrier_semaphore()

    def greet(k, carry):
        pl.semaphore_signal(barrier, inc=1, device_id=where_is(lax.rem(me + k, n)), device_id_type=MESH)
        return carry

    lax.fori_loop(1, n, greet, 0)
    pl.semaphore_wait(barrier, n - 1)

    def to_right(e, src):
        return pltpu.make_async_remote_copy(
            src_ref=src, dst_ref=in_l.at[e], send_sem=hs_r.at[e], recv_sem=hr_l.at[e],
            device_id=where_is(lax.rem(me + 1, n)), device_id_type=MESH,
        )

    def to_left(e, src):
        return pltpu.make_async_remote_copy(
            src_ref=src, dst_ref=in_r.at[e], send_sem=hs_l.at[e], recv_sem=hr_r.at[e],
            device_id=where_is(lax.rem(me + n - 1, n)), device_id_type=MESH,
        )

    def send_halo(e, src_l, src_r):
        @pl.when(me > 0)
        def _():
            to_left(e, src_l).start()

        @pl.when(me < n - 1)
        def _():
            to_right(e, src_r).start()

    def wait_halo(e):
        @pl.when(me > 0)
        def _():
            to_right(e, out_r.at[0]).wait_recv()

        @pl.when(me < n - 1)
        def _():
            to_left(e, out_l.at[0]).wait_recv()

    def wait_sent(e):
        @pl.when(me > 0)
        def _():
            to_left(e, out_l.at[0]).wait_send()

        @pl.when(me < n - 1)
        def _():
            to_right(e, out_r.at[0]).wait_send()

    def rows_below(first, count):
        return lax.broadcasted_iota(jnp.int32, (count, nc), 0) + first < off

    def folded_halo(e, first, count):
        mask = rows_below(first, count)
        right = in_r[e, pl.ds(first, count), :] if first + count <= span else jnp.zeros((count, nc), F32)
        left = in_l[e, pl.ds(first - low, count), :] if first >= low else jnp.zeros((count, nc), F32)
        return jnp.where(mask, right, left)

    def folded(e):
        return jnp.concatenate([folded_halo(e, i * low, low) for i in range(slab // low)], axis=0)

    def apply_block(src):
        twice[0:width, :] = src[...]
        twice[width:, :] = src[...]
        window = twice[pl.ds(off, width), :]
        hi = window.astype(BF16)
        vec[:, :nc] = hi
        vec[:, nc:] = (window - hi.astype(F32)).astype(BF16)

        def rows(i, carry):
            at = pl.ds(pl.multiple_of(i * BLOCK, BLOCK), BLOCK)
            both = jnp.dot(s_hi[at, :], vec[...], preferred_element_type=F32)
            rest = jnp.dot(s_lo[at, :], vec[:, :nc], preferred_element_type=F32)
            result = both[:, :nc] + (both[:, nc:] + rest)
            twice[at, :] = result
            twice[pl.ds(pl.multiple_of(width + i * BLOCK, BLOCK), BLOCK), :] = result
            return carry

        lax.fori_loop(0, width // BLOCK, rows, 0)

    def folded_product():
        return twice[pl.ds(width - off, width), :]

    def send_parts(e, k, product):
        mask = rows_below(0, slab)
        head = product[:slab]
        out_l[k] = jnp.where(mask, 0.0, head)[low:]
        out_r[k] = jnp.where(mask, head, 0.0)[:span]
        send_halo(e, out_l.at[k], out_r.at[k])

    def assemble(e, product):
        wait_halo(e)
        left = in_l[e]
        right = in_r[e]
        mine = product[slab:]
        return jnp.concatenate(
            [
                mine[:low] + left[:low],
                mine[low:span] + (left[low:] + right[: span - low]),
                mine[span:] + right[span - low :],
            ],
            axis=0,
        )

    def reduce_start(r, value):
        rows = value.shape[0]
        p = rows // n
        for i in range(n):
            part[r][i] = value[i * p : (i + 1) * p]

        def send(k, carry):
            peer = lax.rem(me + k, n)
            pltpu.make_async_remote_copy(
                src_ref=part[r].at[peer], dst_ref=fold[r].at[me], send_sem=fold_s.at[r],
                recv_sem=fold_r.at[r], device_id=where_is(peer), device_id_type=MESH,
            ).start()
            return carry

        lax.fori_loop(1, n, send, 0)
        fold[r][me] = part[r][me]

    def reduce_turn(r):
        arrived = fold[r].at[pl.ds(0, n - 1)]
        pltpu.make_async_copy(arrived, arrived, fold_r.at[r]).wait()
        total[r][me] = jnp.sum(fold[r][...], axis=0)

        def send(k, carry):
            peer = lax.rem(me + k, n)
            pltpu.make_async_remote_copy(
                src_ref=total[r].at[me], dst_ref=total[r].at[me], send_sem=tot_s.at[r],
                recv_sem=tot_r.at[r], device_id=where_is(peer), device_id_type=MESH,
            ).start()
            return carry

        lax.fori_loop(1, n, send, 0)

    def reduce_end(r):
        arrived = total[r].at[pl.ds(0, n - 1)]
        pltpu.make_async_copy(arrived, arrived, tot_r.at[r]).wait()
        p = total[r].shape[1]
        for i in range(n):
            m_ref[i * p : (i + 1) * p, :] = total[r][i]
        return m_ref[: n * p, :]

    def scal_start(it):
        scal_all[it, me] = scal_in[it]

        def send(k, carry):
            peer = lax.rem(me + k, n)
            pltpu.make_async_remote_copy(
                src_ref=scal_in.at[it], dst_ref=scal_all.at[it, me], send_sem=scal_s.at[it],
                recv_sem=scal_r.at[it], device_id=where_is(peer), device_id_type=MESH,
            ).start()
            return carry

        lax.fori_loop(1, n, send, 0)

    def scal_end(it):
        arrived = scal_all.at[it, pl.ds(0, n - 1)]
        pltpu.make_async_copy(arrived, arrived, scal_r.at[it]).wait()
        sums = jnp.sum(scal_all[it], axis=0)
        return sums[0:1], sums[1:2], sums[2:3]

    send_halo(0, basis_ref.at[pl.ds(0, span)], basis_ref.at[pl.ds(low, span)])
    basis_t[...] = basis_ref[...].T
    both = jnp.concatenate([basis_ref[...], right_ref[...]], axis=1)
    local = dot(basis_t[...], both)
    reduce_start(0, jnp.concatenate([local[:, :nc], local[:, nc:]], axis=0))

    def split(i, carry):
        slot = lax.rem(i, SLOTS)
        fetch(i, slot).wait()
        at = pl.ds(pl.multiple_of(i * CHUNK, CHUNK), CHUNK)
        value = stage[slot]
        hi = value.astype(BF16)
        s_hi[at, :] = hi
        s_lo[at, :] = (value - hi.astype(F32)).astype(BF16)

        @pl.when(i + SLOTS < chunks)
        def _():
            fetch(i + SLOTS, slot).start()

        return carry

    lax.fori_loop(0, chunks, split, 0)
    reduce_turn(0)

    wait_halo(0)
    basis_w[0:slab, :] = folded(0)
    basis_w[slab:, :] = basis_ref[...]
    apply_block(basis_w)
    product = folded_product()
    send_parts(2, 0, product)
    fc_own[...] = assemble(2, product)
    send_halo(3, fc_own.at[pl.ds(0, span)], fc_own.at[pl.ds(low, span)])
    reduce_start(1, dot(basis_t[...], fc_own[...]))
    fc_t[...] = fc_own[...].T
    gram = reduce_end(0)
    sweep[...] = gram[:nc]
    right_coarse = gram[nc:]
    reduce_turn(1)
    send_halo(1, right_ref.at[pl.ds(0, span)], right_ref.at[pl.ds(low, span)])

    lanes = lax.broadcasted_iota(jnp.int32, (nc, nc), 1)
    subs = lax.broadcasted_iota(jnp.int32, (nc, nc), 0)

    def eliminate(a, k, row, col, p):
        here = lanes == k
        inverse = 1.0 / p
        scaled = row * inverse
        new = a - col * scaled
        new = jnp.where(here, col * inverse, new)
        return jnp.where(subs == k, jnp.where(here, -inverse, scaled), new), scaled, inverse

    def pick(row, k):
        return jnp.sum(jnp.where(lanes[:1] == k, row, 0.0), axis=1, keepdims=True)

    def pivot(half, a):
        k = 2 * half
        row1, row2 = sweep[pl.ds(k, 1), :], sweep[pl.ds(k + 1, 1), :]
        col1 = jnp.sum(jnp.where(lanes == k, a, 0.0), axis=1, keepdims=True)
        col2 = jnp.sum(jnp.where(lanes == k + 1, a, 0.0), axis=1, keepdims=True)
        p1, cross, p2 = pick(row1, k), pick(row1, k + 1), pick(row2, k + 1)
        a, scaled, inverse = eliminate(a, k, row1, col1, p1)
        ratio = cross * inverse
        row2 = jnp.where(lanes[:1] == k, ratio, row2 - cross * scaled)
        col2 = jnp.where(subs[:, :1] == k, ratio, col2 - col1 * ratio)
        a, _, _ = eliminate(a, k + 1, row2, col2, p2 - cross * ratio)
        sweep[...] = a
        return a

    ginv = -lax.fori_loop(0, nc // 2, pivot, sweep[...])

    y0 = dot(ginv, load_ref[...])
    lam_ref[...] = dot(basis_ref[...], y0)
    cfc = reduce_end(1)
    amp = dot(ginv, right_coarse - dot(cfc, y0))
    wait_halo(1)
    wait_halo(3)
    right_w[0:slab, :] = folded(1)
    right_w[slab:, :] = right_ref[...]
    fc_w[0:slab, :] = folded(3)
    fc_w[slab:, :] = fc_own[...]
    z[...] = right_w[...] - dot(fc_w[...], y0) - dot(basis_w[...], amp)

    energy = curvature = coarse_image = None
    for it in range(ITERS):
        last = it == ITERS - 1
        reduce_start(2 + it, dot(fc_t[...], z[slab:, :]))
        apply_block(z)
        product = folded_product()
        e = 4 + 2 * it
        if not last:
            send_parts(e, 1 + it, product)
        scal_in[it, 0:1] = jnp.sum(z[...] * product, axis=0, keepdims=True)
        scal_in[it, 1:2] = jnp.sum(z[slab:, :] * z[slab:, :], axis=0, keepdims=True)
        if it == 0:
            scal_in[it, 2:3] = jnp.zeros((1, nc), F32)
        else:
            scal_in[it, 2:3] = jnp.sum(z[...] * p_old[...], axis=0, keepdims=True)
        scal_in[it, 3:4] = jnp.zeros((1, nc), F32)
        scal_start(it)
        reduce_turn(2 + it)
        if not last:
            own[it] = assemble(e, product)
            send_halo(e + 1, own.at[it, pl.ds(0, span)], own.at[it, pl.ds(low, span)])
        curved, energy_now, crossed = scal_end(it)
        coarse_now = reduce_end(2 + it)
        if it == 0:
            d[...] = z[slab:, :]
            curvature = curved
            coarse_image = coarse_now
            if not last:
                p_old[...] = product
        else:
            beta = energy_now / energy
            d[...] = z[slab:, :] + beta * d[...]
            curvature = curved + beta * (2.0 * crossed + beta * curvature)
            coarse_image = coarse_now + beta * coarse_image
            if not last:
                p_old[...] = product + beta * p_old[...]
        energy = energy_now
        step = energy / curvature
        lam_ref[...] += step * d[...]
        shift = dot(ginv, coarse_image)
        amp = amp - step * shift
        if not last:
            wait_halo(e + 1)
            whole = jnp.concatenate([folded(e + 1), own[it]], axis=0)
            if it > 0:
                whole = whole + beta * image_old[...]
            image_old[...] = whole
            z[...] = z[...] - step * (whole - dot(basis_w[...], shift))
    amp_ref[...] = amp

    for e in range(EXCHANGES):
        wait_sent(e)
    for r in range(REDUCES):
        sent = fold[r].at[pl.ds(0, n - 1)]
        pltpu.make_async_copy(sent, sent, fold_s.at[r]).wait()
        sent = total[r].at[pl.ds(0, n - 1)]
        pltpu.make_async_copy(sent, sent, tot_s.at[r]).wait()
    for it in range(ITERS):
        sent = scal_all.at[it, pl.ds(0, n - 1)]
        pltpu.make_async_copy(sent, sent, scal_s.at[it]).wait()


def entry(nx, ny, groups, *refs):
    fixed = refs[: groups[0]]
    rest = refs[groups[0] :]
    part, rest = rest[:REDUCES], rest[REDUCES:]
    fold, rest = rest[:REDUCES], rest[REDUCES:]
    total, rest = rest[:REDUCES], rest[REDUCES:]
    kernel(nx, ny, *fixed, part, fold, total, *rest)


def solution(mesh):
    nx, ny = mesh.shape["gx"], mesh.shape["gy"]
    n = nx * ny

    def local(schur_blocks, offsets, right_side, coarse_basis, coarse_load):
        slab, r = right_side.shape
        nc = coarse_basis.shape[1]
        width = schur_blocks.shape[1]
        span = slab - slab // 4
        row_counts = [2 * nc] + [nc] * (REDUCES - 1)

        def pieces():
            return [pltpu.VMEM((n, rows // n, r), F32) for rows in row_counts]

        vmem = pl.BlockSpec(memory_space=pltpu.VMEM)
        fixed = [
            pltpu.VMEM((SLOTS, CHUNK, width), F32),
            pltpu.VMEM((width, width), BF16),
            pltpu.VMEM((width, width), BF16),
            pltpu.VMEM((width, 2 * r), BF16),
            pltpu.VMEM((2 * width, r), F32),
            pltpu.VMEM((width, nc), F32),
            pltpu.VMEM((nc, slab), F32),
            pltpu.VMEM((slab, nc), F32),
            pltpu.VMEM((width, nc), F32),
            pltpu.VMEM((nc, slab), F32),
            pltpu.VMEM((width, r), F32),
            pltpu.VMEM((width, r), F32),
            pltpu.VMEM((slab, r), F32),
            pltpu.VMEM((width, r), F32),
            pltpu.VMEM((width, r), F32),
            pltpu.VMEM((ITERS - 1, slab, r), F32),
            pltpu.VMEM((ITERS, span, r), F32),
            pltpu.VMEM((ITERS, span, r), F32),
            pltpu.VMEM((EXCHANGES, span, r), F32),
            pltpu.VMEM((EXCHANGES, span, r), F32),
        ]
        dma = pltpu.SemaphoreType.DMA
        rest = [
            pltpu.VMEM((2 * nc, r), F32),
            pltpu.VMEM((nc, nc), F32),
            pltpu.VMEM((ITERS, 4, r), F32),
            pltpu.VMEM((ITERS, n, 4, r), F32),
            dma((SLOTS,)),
            dma((EXCHANGES,)), dma((EXCHANGES,)), dma((EXCHANGES,)), dma((EXCHANGES,)),
            dma((REDUCES,)), dma((REDUCES,)), dma((REDUCES,)), dma((REDUCES,)),
            dma((ITERS,)), dma((ITERS,)),
        ]
        return pl.pallas_call(
            functools.partial(entry, nx, ny, (7 + len(fixed),)),
            out_shape=(
                jax.ShapeDtypeStruct((slab, r), F32),
                jax.ShapeDtypeStruct((nc, r), F32),
            ),
            in_specs=[
                pl.BlockSpec(memory_space=pltpu.SMEM),
                pl.BlockSpec(memory_space=pl.ANY),
                vmem, vmem, vmem,
            ],
            out_specs=(vmem, vmem),
            scratch_shapes=fixed + pieces() + pieces() + pieces() + rest,
            compiler_params=pltpu.CompilerParams(
                collective_id=0, has_side_effects=True, vmem_limit_bytes=60 * 1024 * 1024
            ),
            name="projected_cg",
        )(offsets, schur_blocks[0], right_side, coarse_basis, coarse_load)

    in_specs = (
        P(("gx", "gy"), None, None),
        P(("gx", "gy")),
        P(("gx", "gy"), None),
        P(("gx", "gy"), None),
        P(),
    )
    out_specs = (P(("gx", "gy"), None), P())
    return jax.shard_map(local, mesh=mesh, in_specs=in_specs, out_specs=out_specs, check_vma=False)
```
